128 devices in a mesh: dp: 4 (over z_hi, core), ctx: 32 (over z_lo, y, x).
Axes of the slice: x: 4, y: 4, z: 4 (z_hi: 2, z_lo: 2; z = z_hi * 2 + z_lo), core: 2. Of those that a mesh axis runs over, the one named last changes fastest.
Arguments:
- queries: bfloat16 [4, 4096, 4096], P('dp', 'ctx'), may hold values from -41 to 41
- attn_keys: bfloat16 [4, 4096, 4096], P('dp', 'ctx'), may hold values from -6 to 6
- attn_values: bfloat16 [4, 4096, 4096], P('dp', 'ctx'), may hold values from -6 to 6
- outer_gate: bfloat16 [4, 4096, 4096], P('dp', 'ctx'), may hold values from -6 to 6
- inner_gate: bfloat16 [4, 4096, 4096], P('dp', 'ctx'), may hold values from -6 to 6
- conv_filter: bfloat16 [256, 128], replicated, may hold values from -0.5 to 0.5
- grad_mixed: bfloat16 [4, 4096, 4096], P('dp', 'ctx'), may hold values from -6 to 6
Outputs:
- block_out: bfloat16 [4, 4096, 4096], P('dp', 'ctx')
- grad_queries: bfloat16 [4, 4096, 4096], P('dp', 'ctx')
- grad_keys: bfloat16 [4, 4096, 4096], P('dp', 'ctx')
- grad_values: bfloat16 [4, 4096, 4096], P('dp', 'ctx')
- grad_outer: bfloat16 [4, 4096, 4096], P('dp', 'ctx')
- grad_inner: bfloat16 [4, 4096, 4096], P('dp', 'ctx')
- grad_filter: float32 [256, 128], replicated
The draws below stay inside these ranges and needn't reach their ends.
All inputs are finite; a program needn't handle non-finite values.
Results may differ from the reference program's by a relative error of at most 0.007.
Values may be sent and summed in bfloat16 or wider, within the bound.
A program may use at most 192 MiB of HBM per device.

```python
import jax
import jax.numpy as jnp
from jax import lax

HEADS = 32
HEAD_DIM = 128
GROUP_CH = 16
KERNEL = 128
BATCH = 4
TOKENS = 4096
CHANNELS = 4096
GROUPS = 256


def draw_pair(key):
    base_key = jax.random.fold_in(key, 11)
    key_query, key_key = jax.random.split(base_key)
    array_shape = (BATCH, TOKENS, CHANNELS)
    key_rows = jax.random.truncated_normal(key_key, -6.0, 6.0, array_shape, jnp.float32)
    query_rows = jax.random.truncated_normal(key_query, -6.0, 6.0, array_shape, jnp.float32)
    return (query_rows.astype(jnp.bfloat16), key_rows.astype(jnp.bfloat16))


def draw_queries(key, part):
    return draw_pair(key)[0]


def draw_attn_keys(key, part):
    return draw_pair(key)[1]


def block_levels(rng, extent, cuts, least, top_value):
    level, own = 1.0, jax.random.fold_in(rng, 6)
    for dim, shards_of in cuts:
        steps = jnp.exp(jax.random.uniform(jax.random.fold_in(own, dim), (shards_of,), jnp.float32, least / len(cuts), top_value / len(cuts)))
        level = level * jnp.repeat(steps, extent[dim] // shards_of).reshape([-1 if axis == dim else 1 for axis in range(len(extent))])
    return level


def bell_draw(own_key, dims, width, bound, shards=(), kind=jnp.bfloat16):
    result = jax.random.normal(own_key, dims, jnp.float32) * width
    if len(shards) > 0:
        result = block_levels(own_key, dims, shards, -0.22, 0.18) * result
    return jnp.clip(result, min=-bound, max=bound).astype(kind)


def setup_inputs(seed: int = 0) -> dict:
    arg_keys = jax.random.split(jax.random.key(seed), 8)
    return {
        "queries": draw_queries(jax.random.fold_in(arg_keys[7], 71), 0),
        "attn_keys": draw_attn_keys(jax.random.fold_in(arg_keys[7], 71), 0),
        "attn_values": bell_draw(arg_keys[2], (BATCH, TOKENS, CHANNELS), 1.0, 6.0, ((0, 4), (1, 32))),
        "outer_gate": bell_draw(arg_keys[3], (BATCH, TOKENS, CHANNELS), 1.0, 6.0, ((0, 4), (1, 32))),
        "inner_gate": bell_draw(arg_keys[4], (BATCH, TOKENS, CHANNELS), 1.0, 6.0, ((0, 4), (1, 32))),
        "conv_filter": bell_draw(arg_keys[5], (GROUPS, KERNEL), KERNEL ** -0.5, 0.5),
        "grad_mixed": bell_draw(arg_keys[6], (BATCH, TOKENS, CHANNELS), 1.0, 6.0, ((0, 4), (1, 32))),
    }


def split_heads(array):
    shaped = array.reshape(BATCH, TOKENS, HEADS, HEAD_DIM)
    return shaped.transpose(0, 2, 1, 3).reshape(BATCH * HEADS, TOKENS, HEAD_DIM)


def join_heads(array):
    shaped = array.reshape(BATCH, HEADS, TOKENS, HEAD_DIM)
    return shaped.transpose(0, 2, 1, 3).reshape(BATCH, TOKENS, HEADS * HEAD_DIM)


def head_probs(query_rows, key_rows):
    scores = jnp.dot(query_rows.astype(jnp.float32), key_rows.astype(jnp.float32).T, preferred_element_type=jnp.float32) * (HEAD_DIM ** -0.5)
    position = jnp.arange(TOKENS, dtype=jnp.int32)
    causal = position[None, :] <= position[:, None]
    scores = jnp.where(causal, scores, -jnp.inf)
    row_max = jnp.max(scores, axis=1, keepdims=True)
    exponent = jnp.exp(scores - row_max)
    return exponent / jnp.sum(exponent, axis=1, keepdims=True)


def head_forward(items):
    query_rows, key_rows, value_rows = items
    attn_probs = head_probs(query_rows, key_rows)
    probs_low = lax.optimization_barrier(attn_probs.astype(jnp.bfloat16)).astype(jnp.float32)
    return jnp.dot(probs_low, value_rows.astype(jnp.float32), preferred_element_type=jnp.float32).astype(jnp.bfloat16)


def head_backward(items):
    query_rows, key_rows, value_rows, grad_rows = items
    softmax_scale = HEAD_DIM ** -0.5
    attn_probs = head_probs(query_rows, key_rows)
    probs_low = lax.optimization_barrier(attn_probs.astype(jnp.bfloat16)).astype(jnp.float32)
    grad_probs = jnp.dot(grad_rows.astype(jnp.float32), value_rows.astype(jnp.float32).T, preferred_element_type=jnp.float32)
    row_inner = jnp.sum(attn_probs * grad_probs, axis=1, keepdims=True)
    grad_scores = lax.optimization_barrier((attn_probs * (grad_probs - row_inner)).astype(jnp.bfloat16)).astype(jnp.float32)
    grad_q = (jnp.dot(grad_scores, key_rows.astype(jnp.float32), preferred_element_type=jnp.float32) * softmax_scale).astype(jnp.bfloat16)
    grad_k = (jnp.dot(grad_scores.T, query_rows.astype(jnp.float32), preferred_element_type=jnp.float32) * softmax_scale).astype(jnp.bfloat16)
    grad_v = jnp.dot(probs_low.T, grad_rows.astype(jnp.float32), preferred_element_type=jnp.float32).astype(jnp.bfloat16)
    return grad_q, grad_k, grad_v


def reference(queries, attn_keys, attn_values, outer_gate, inner_gate, conv_filter, grad_mixed):
    heads_q = split_heads(queries)
    heads_k = split_heads(attn_keys)
    heads_v = split_heads(attn_values)
    attended = join_heads(lax.map(head_forward, (heads_q, heads_k, heads_v)))
    gated_in = (inner_gate.astype(jnp.float32) * attended.astype(jnp.float32)).astype(jnp.bfloat16)
    per_channel = jnp.repeat(conv_filter.astype(jnp.float32), GROUP_CH, axis=0)
    padded_in = jnp.pad(gated_in.astype(jnp.float32), ((0, 0), (KERNEL - 1, 0), (0, 0)))

    def forward_tap(tap_index, running):
        window = lax.dynamic_slice_in_dim(padded_in, KERNEL - 1 - tap_index, TOKENS, 1)
        return running + per_channel[:, tap_index] * window

    filtered = lax.fori_loop(0, KERNEL, forward_tap, jnp.zeros((BATCH, TOKENS, CHANNELS), jnp.float32))
    block_out = (outer_gate.astype(jnp.float32) * filtered).astype(jnp.bfloat16)
    grad_filtered = (grad_mixed.astype(jnp.float32) * outer_gate.astype(jnp.float32)).astype(jnp.bfloat16)
    grad_outer = (grad_mixed.astype(jnp.float32) * filtered).astype(jnp.bfloat16)
    padded_grad = jnp.pad(grad_filtered.astype(jnp.float32), ((0, 0), (0, KERNEL - 1), (0, 0)))

    def backward_tap(tap_index, running):
        window = lax.dynamic_slice_in_dim(padded_grad, tap_index, TOKENS, 1)
        return running + per_channel[:, tap_index] * window

    grad_gated = lax.fori_loop(0, KERNEL, backward_tap, jnp.zeros((BATCH, TOKENS, CHANNELS), jnp.float32))

    def filter_tap(tap_index):
        window = lax.dynamic_slice_in_dim(padded_in, KERNEL - 1 - tap_index, TOKENS, 1)
        summed = jnp.sum(grad_filtered.astype(jnp.float32) * window, axis=(0, 1))
        return summed.reshape(GROUPS, GROUP_CH).sum(axis=1)

    grad_filter = lax.map(filter_tap, jnp.arange(KERNEL, dtype=jnp.int32)).T
    grad_inner = (grad_gated * attended.astype(jnp.float32)).astype(jnp.bfloat16)
    grad_attended = (grad_gated * inner_gate.astype(jnp.float32)).astype(jnp.bfloat16)
    grads = lax.map(head_backward, (heads_q, heads_k, heads_v, split_heads(grad_attended)))
    return (block_out, join_heads(grads[0]), join_heads(grads[1]), join_heads(grads[2]), grad_outer, grad_inner, grad_filter)
```

```python
import functools
import math

import jax
import jax.numpy as jnp
from jax import lax
from jax.experimental import pallas as pl
from jax.experimental.pallas import tpu as pltpu
from jax.sharding import PartitionSpec as P

F32 = jnp.float32
BF16 = jnp.bfloat16
MESH = pl.DeviceIdType.MESH
LANES = 128
QUERY_BLOCK = 1024
KEY_ROWS = 256
VMEM_BYTES = 62 * 2**20


def dot(a, b):
    return jnp.dot(a, b, preferred_element_type=F32)


def rows_of(index, size):
    return pl.ds(pl.multiple_of(index * size, size), size)


def fold(x, op):
    return op(x.reshape(x.shape[0] // 8, 8, x.shape[1]), axis=0)


def ctx_peer(me, step):
    x = (me + step) % 4
    y = (me // 4 + step // 4) % 4
    z = (me // 16 + step // 16) % 2
    return z * 16 + y * 4 + x


def greet(devices):
    barrier = pltpu.get_barrier_semaphore()

    def signal(step, carry):
        peer = ctx_peer(lax.axis_index("ctx"), step)
        pl.semaphore_signal(barrier, inc=1, device_id={"ctx": peer}, device_id_type=MESH)
        return carry

    lax.fori_loop(1, devices, signal, 0)
    return barrier


def gather_heads_kernel(devices, q, k, v, og, ig, gm, qh, kh, vh, gfh, igh, gf, send_sem, recv_sem, own_sem):
    me = lax.axis_index("ctx")
    local = q.shape[0]
    barrier = greet(devices)

    def gate(index, carry):
        at = rows_of(index, LANES)
        gf[:, at] = (gm[:, at].astype(F32) * og[:, at].astype(F32)).astype(BF16)
        return carry

    lax.fori_loop(0, devices, gate, 0)
    pl.semaphore_wait(barrier, devices - 1)
    pairs = ((q, qh), (k, kh), (v, vh), (ig, igh), (gf, gfh))
    mine = rows_of(me, local)
    own = [
        pltpu.make_async_copy(src.at[:, rows_of(me, LANES)], dst.at[mine, :], own_sem.at[n])
        for n, (src, dst) in enumerate(pairs)
    ]
    for n, (src, dst) in enumerate(pairs):

        def send(step, carry, n=n, src=src, dst=dst):
            peer = ctx_peer(me, step)
            pltpu.make_async_remote_copy(
                src_ref=src.at[:, rows_of(peer, LANES)],
                dst_ref=dst.at[mine, :],
                send_sem=send_sem.at[n],
                recv_sem=recv_sem.at[n],
                device_id={"ctx": peer},
                device_id_type=MESH,
            ).start()
            return carry

        lax.fori_loop(1, devices, send, 0)
    for copy in own:
        copy.start()
    for n, (_, dst) in enumerate(pairs):
        own[n].wait()
        others = dst.at[pl.ds(0, (devices - 1) * local), :]
        pltpu.make_async_copy(others, others, recv_sem.at[n]).wait()
        pltpu.make_async_copy(others, others, send_sem.at[n]).wait()


def gather_heads(devices, q, k, v, og, ig, gm):
    local, channels = q.shape
    hbm = pl.BlockSpec(memory_space=pl.ANY)
    vmem = pl.BlockSpec(memory_space=pltpu.VMEM)
    head = jax.ShapeDtypeStruct((local * devices, LANES), BF16)
    return pl.pallas_call(
        functools.partial(gather_heads_kernel, devices),
        out_shape=(head,) * 5,
        in_specs=[hbm, hbm, hbm, vmem, hbm, vmem],
        out_specs=(hbm,) * 5,
        scratch_shapes=[pltpu.VMEM((local, channels), BF16)] + [pltpu.SemaphoreType.DMA((5,))] * 3,
        compiler_params=pltpu.CompilerParams(collective_id=0, has_side_effects=True),
        name="gather_heads",
    )(q, k, v, og, ig, gm)


def scatter_heads_kernel(devices, parts, *refs):
    sources, partial = refs[:5], refs[5]
    targets, partials = refs[6:11], refs[11]
    send_sem, recv_sem, own_sem, send_small, recv_small, own_small = refs[12:]
    me, part = lax.axis_index("ctx"), lax.axis_index("dp")
    local = targets[0].shape[0]
    few = partial.shape[0]
    barrier = pltpu.get_barrier_semaphore()

    def signal(step, carry):
        peer = ctx_peer(me, step // parts)
        other = (part + step) % parts
        pl.semaphore_signal(barrier, inc=1, device_id={"ctx": peer, "dp": other}, device_id_type=MESH)
        return carry

    lax.fori_loop(1, devices * parts, signal, 0)
    pl.semaphore_wait(barrier, devices * parts - 1)
    mine = rows_of(me, LANES)
    small = partials.at[rows_of(part * devices + me, few), :]

    def send_partial(step, carry):
        peer = ctx_peer(me, step // parts)
        other = (part + step) % parts
        pltpu.make_async_remote_copy(
            src_ref=partial,
            dst_ref=small,
            send_sem=send_small,
            recv_sem=recv_small,
            device_id={"ctx": peer, "dp": other},
            device_id_type=MESH,
        ).start()
        return carry

    lax.fori_loop(1, devices * parts, send_partial, 0)
    own = [
        pltpu.make_async_copy(src.at[rows_of(me, local), :], dst.at[:, mine], own_sem.at[n])
        for n, (src, dst) in enumerate(zip(sources, targets))
    ]
    for n, (src, dst) in enumerate(zip(sources, targets)):

        def send(step, carry, n=n, src=src, dst=dst):
            peer = ctx_peer(me, step)
            pltpu.make_async_remote_copy(
                src_ref=src.at[rows_of(peer, local), :],
                dst_ref=dst.at[:, mine],
                send_sem=send_sem.at[n],
                recv_sem=recv_sem.at[n],
                device_id={"ctx": peer},
                device_id_type=MESH,
            ).start()
            return carry

        lax.fori_loop(1, devices, send, 0)
    for copy in own:
        copy.start()
    own_part = pltpu.make_async_copy(partial, small, own_small)
    own_part.start()
    for n, dst in enumerate(targets):
        own[n].wait()
        others = dst.at[:, pl.ds(0, (devices - 1) * LANES)]
        pltpu.make_async_copy(others, others, recv_sem.at[n]).wait()
        pltpu.make_async_copy(others, others, send_sem.at[n]).wait()
    own_part.wait()
    others = partials.at[pl.ds(0, (devices * parts - 1) * few), :]
    for sem in (recv_small, send_small):
        pltpu.make_async_copy(others, others, sem).wait()


def scatter_heads(devices, parts, arrays, partial):
    tokens, width = arrays[0].shape
    hbm = pl.BlockSpec(memory_space=pl.ANY)
    rows = jax.ShapeDtypeStruct((tokens // devices, width * devices), BF16)
    few = partial.shape[0]
    return pl.pallas_call(
        functools.partial(scatter_heads_kernel, devices, parts),
        out_shape=(rows,) * 5 + (jax.ShapeDtypeStruct((parts * devices * few, partial.shape[1]), F32),),
        in_specs=[hbm] * 6,
        out_specs=(hbm,) * 6,
        scratch_shapes=[pltpu.SemaphoreType.DMA((5,))] * 3 + [pltpu.SemaphoreType.DMA] * 3,
        compiler_params=pltpu.CompilerParams(collective_id=1, has_side_effects=True),
        name="scatter_heads",
    )(*arrays, partial)


def head_kernel(
    groups, q, k, v, gf, ig, w,
    dq, dk, dv, gi, fil, gw,
    wf, gfp, xp, g, gg, later, earlier, kt, vt, s_all, dp_all, dka, dva, ot, dqt, corr,
):
    tokens, width = q.shape
    tile = later.shape[1] // 2
    per = width // groups
    block, part = QUERY_BLOCK, KEY_ROWS
    blocks = tokens // block
    pieces = block // part
    scale = width**-0.5
    factor = scale * math.log2(math.e)
    head = lax.axis_index("ctx")

    wf[...] = w[...].astype(F32)
    taps = wf[rows_of(head, groups), :]
    row = lax.broadcasted_iota(jnp.int32, (tile, tile), 0)
    col = lax.broadcasted_iota(jnp.int32, (tile, tile), 1)
    for n in range(groups):
        ring = jnp.broadcast_to(taps[n : n + 1, :], (tile, tile))
        shift = 1
        while shift < tile:
            ring = jnp.where((row & shift) != 0, pltpu.roll(ring, shift, 1), ring)
            shift *= 2
        upper = jnp.where(col >= row, ring, 0.0)
        lower = jnp.where(col < row, ring, 0.0)
        at = pl.ds(n * tile, tile)
        later[at, :tile] = upper.astype(BF16)
        later[at, tile:] = lower.astype(BF16)
        earlier[at, :tile] = lower.T.astype(BF16)
        earlier[at, tile:] = upper.T.astype(BF16)
    gfp[:tokens, :] = gf[...]
    gfp[tokens:, :] = jnp.zeros((tile, width), BF16)
    xp[:tile, :] = jnp.zeros((tile, width), BF16)

    lane_group = lax.broadcasted_iota(jnp.int32, (tile, width), 1) // per

    def convolved(matrix, signal, first):
        window = jnp.concatenate(
            [signal[pl.ds(pl.multiple_of(first + n * tile, tile), 2 * tile), :] for n in range(2)],
            axis=1,
        )
        result = [jnp.zeros((tile, width), F32)] * 2
        for n in range(groups):
            product = dot(matrix[pl.ds(n * tile, tile), :], window)
            for m in range(2):
                result[m] = jnp.where(lane_group == n, product[:, m * width : (m + 1) * width], result[m])
        return result

    def conv_back(index, carry):
        for m, value in enumerate(convolved(later, gfp, index * 2 * tile)):
            at = pl.ds(pl.multiple_of(index * 2 * tile + m * tile, tile), tile)
            gg[at, :] = value
            g[at, :] = (value * ig[at, :].astype(F32)).astype(BF16)
        return carry

    lax.fori_loop(0, tokens // (2 * tile), conv_back, 0)

    def turn(index, carry):
        at = rows_of(index, part)
        kt[index] = k[at, :].T
        vt[index] = v[at, :].T
        return carry

    lax.fori_loop(0, tokens // part, turn, 0)

    def query_block(i, carry):
        rows = rows_of(i, block)
        qb, gb = q[rows, :], g[rows, :]
        q_t, g_t = qb.T, gb.T

        def key_rows(j, r):
            return pl.ds(pl.multiple_of(j * block + r * part, part), part)

        def widen(value, skip, fill):
            if skip == 0:
                return value
            return jnp.concatenate([jnp.full((value.shape[0], skip), fill, F32), value], axis=1)

        def scores(j, top, diagonal=False):
            for r in range(pieces):
                at = key_rows(j, r)
                skip = r * part if diagonal else 0
                s = dot(k[at, :], q_t[:, skip:])
                if diagonal:
                    key_id = lax.broadcasted_iota(jnp.int32, s.shape, 0)
                    query_id = lax.broadcasted_iota(jnp.int32, s.shape, 1)
                    s = jnp.where(key_id <= query_id, s, -jnp.inf)
                s_all[at, skip:] = s
                top = jnp.maximum(top, widen(fold(s, jnp.max), skip, -jnp.inf))
            return top

        top = lax.fori_loop(0, i, scores, jnp.full((8, block), -jnp.inf, F32))
        top = jnp.max(scores(i, top, True), axis=0, keepdims=True)

        def probs(j, sums, diagonal=False):
            total, inner = sums
            for r in range(pieces):
                at = key_rows(j, r)
                skip = r * part if diagonal else 0
                p = jnp.exp2((s_all[at, skip:] - top[:, skip:]) * factor)
                grad_p = dot(v[at, :], g_t[:, skip:])
                s_all[at, skip:] = p
                dp_all[at, skip:] = grad_p
                total = total + widen(fold(p, jnp.sum), skip, 0.0)
                inner = inner + widen(fold(p * grad_p, jnp.sum), skip, 0.0)
            return total, inner

        none = jnp.zeros((8, block), F32)
        total, inner = probs(i, lax.fori_loop(0, i, probs, (none, none)), True)
        inverse = 1.0 / jnp.sum(total, axis=0, keepdims=True)
        inner = jnp.sum(inner, axis=0, keepdims=True) * inverse

        def grads(j, nothing, diagonal=False):
            for r in range(pieces):
                at = key_rows(j, r)
                skip = r * part if diagonal else 0
                p = s_all[at, skip:] * inverse[:, skip:]
                low = p.astype(BF16)
                grad_s = (p * (dp_all[at, skip:] - inner[:, skip:])).astype(BF16)
                value_part = dot(low, gb[skip:, :])
                key_part = dot(grad_s, qb[skip:, :])
                out_part = dot(vt[j * pieces + r], low)
                query_part = dot(kt[j * pieces + r], grad_s)
                if diagonal:
                    dva[at, :] = value_part
                    dka[at, :] = key_part
                else:
                    dva[at, :] += value_part
                    dka[at, :] += key_part
                if diagonal and r == 0:
                    ot[...] = out_part
                    dqt[...] = query_part
                else:
                    ot[:, skip:] += out_part
                    dqt[:, skip:] += query_part
            return nothing

        grads(i, 0, True)
        lax.fori_loop(0, i, grads, 0)
        attended = ot[...].T.astype(BF16).astype(F32)
        dq[rows, :] = (dqt[...] * scale).T.astype(BF16)
        gi[rows, :] = (gg[rows, :] * attended).astype(BF16)
        xp[pl.ds(pl.multiple_of(i * block + tile, tile), block), :] = (
            attended * ig[rows, :].astype(F32)
        ).astype(BF16)
        return carry

    lax.fori_loop(0, blocks, query_block, 0)

    def finish(index, carry):
        at = rows_of(index, part)
        dk[at, :] = (dka[at, :] * scale).astype(BF16)
        dv[at, :] = dva[at, :].astype(BF16)
        return carry

    lax.fori_loop(0, tokens // part, finish, 0)

    row_group = lax.broadcasted_iota(jnp.int32, (width, tile), 0) // per
    corr[...] = jnp.zeros_like(corr)

    def conv_ahead(index, carry):
        for m, value in enumerate(convolved(earlier, xp, index * 2 * tile)):
            at = pl.ds(pl.multiple_of(index * 2 * tile + m * tile, tile), tile)
            fil[at, :] = value.astype(BF16)
        lefts, rights = [], []
        for m in range(2):
            first = pl.multiple_of(index * 2 * tile + m * tile, tile)
            lefts.append(xp[pl.ds(first, 2 * tile), :])
            turned = gfp[pl.ds(first, tile), :].astype(F32).T
            rights.append(
                jnp.concatenate([jnp.where(row_group == n, turned, 0.0) for n in range(groups)], axis=1)
            )
        left = jnp.concatenate(lefts, axis=1)
        right = jnp.concatenate(rights, axis=0).astype(BF16)
        corr[...] += dot(left, right)
        return carry

    lax.fori_loop(0, tokens // (2 * tile), conv_ahead, 0)

    for n in range(groups):
        at = pl.ds(n * tile, tile)
        skewed = jnp.where(col >= row, corr[tile:, at], corr[:tile, at])
        shift = 1
        while shift < tile:
            skewed = jnp.where((row & shift) != 0, pltpu.roll(skewed, tile - shift, 1), skewed)
            shift *= 2
        gw[n : n + 1, :] = jnp.sum(skewed, axis=0, keepdims=True)


def one_head(q, k, v, gf, ig, w, devices):
    tokens, width = q.shape
    groups = w.shape[0] // devices
    tile = w.shape[1]
    head = jax.ShapeDtypeStruct((tokens, width), BF16)
    vmem = pl.BlockSpec(memory_space=pltpu.VMEM)
    part = KEY_ROWS
    return pl.pallas_call(
        functools.partial(head_kernel, groups),
        out_shape=(head,) * 5 + (jax.ShapeDtypeStruct((groups, tile), F32),),
        in_specs=[vmem] * 6,
        out_specs=(vmem,) * 6,
        scratch_shapes=[
            pltpu.VMEM(w.shape, F32),
            pltpu.VMEM((tokens + tile, width), BF16),
            pltpu.VMEM((tokens + tile, width), BF16),
            pltpu.VMEM((tokens, width), BF16),
            pltpu.VMEM((tokens, width), F32),
            pltpu.VMEM((groups * tile, 2 * tile), BF16),
            pltpu.VMEM((groups * tile, 2 * tile), BF16),
            pltpu.VMEM((tokens // part, width, part), BF16),
            pltpu.VMEM((tokens // part, width, part), BF16),
            pltpu.VMEM((tokens, QUERY_BLOCK), F32),
            pltpu.VMEM((tokens, QUERY_BLOCK), F32),
            pltpu.VMEM((tokens, width), F32),
            pltpu.VMEM((tokens, width), F32),
            pltpu.VMEM((width, QUERY_BLOCK), F32),
            pltpu.VMEM((width, QUERY_BLOCK), F32),
            pltpu.VMEM((2 * tile, groups * tile), F32),
        ],
        compiler_params=pltpu.CompilerParams(vmem_limit_bytes=VMEM_BYTES),
        name="one_head",
    )(q, k, v, gf, ig, w)


def results_kernel(
    dq, dk, dv, gi, fil, parts, og, gm, out_block, out_q, out_k, out_v, out_outer, out_inner, out_w
):
    filtered = fil[...].astype(F32)
    out_block[...] = (og[...].astype(F32) * filtered).astype(BF16)
    out_outer[...] = (gm[...].astype(F32) * filtered).astype(BF16)
    out_q[...] = dq[...]
    out_k[...] = dk[...]
    out_v[...] = dv[...]
    out_inner[...] = gi[...]
    out_w[...] = jnp.sum(parts[...], axis=0)


def results(arrays, partials, og, gm):
    rows, channels = og.shape
    steps = 4
    wide = pl.BlockSpec((rows // steps, channels), lambda i: (i, 0))
    n_parts, few, taps = partials.shape
    array = jax.ShapeDtypeStruct((rows, channels), BF16)
    return pl.pallas_call(
        results_kernel,
        grid=(steps,),
        out_shape=(array,) * 6 + (jax.ShapeDtypeStruct((few, taps), F32),),
        in_specs=[wide] * 5
        + [pl.BlockSpec((n_parts, few // steps, taps), lambda i: (0, i, 0))]
        + [wide] * 2,
        out_specs=(wide,) * 6 + (pl.BlockSpec((few // steps, taps), lambda i: (i, 0)),),
        name="results",
    )(*arrays, partials, og, gm)


def on_device(queries, attn_keys, attn_values, outer_gate, inner_gate, conv_filter, grad_mixed):
    devices, parts = lax.axis_size("ctx"), lax.axis_size("dp")
    og, gm = outer_gate[0], grad_mixed[0]
    heads = gather_heads(devices, queries[0], attn_keys[0], attn_values[0], og, inner_gate[0], gm)
    qh, kh, vh, gfh, igh = heads
    *arrays, partial = one_head(qh, kh, vh, gfh, igh, conv_filter, devices)
    *arrays, partials = scatter_heads(devices, parts, arrays, partial)
    partials = partials.reshape(parts, *conv_filter.shape)
    *arrays, grad_filter = results(arrays, partials, og, gm)
    return (*[array[None] for array in arrays], grad_filter)


def solution(mesh):
    spread = P("dp", "ctx", None)
    return jax.shard_map(
        on_device,
        mesh=mesh,
        in_specs=(spread,) * 5 + (P(), spread),
        out_specs=(spread,) * 6 + (P(),),
        check_vma=False,
    )
```

```python
import functools
import math

import jax
import jax.numpy as jnp
from jax import lax
from jax.experimental import pallas as pl
from jax.experimental.pallas import tpu as pltpu
from jax.sharding import PartitionSpec as P

F32 = jnp.float32
BF16 = jnp.bfloat16
MESH = pl.DeviceIdType.MESH
LANES = 128
QUERY_BLOCK = 1024
KEY_ROWS = 256
VMEM_BYTES = 67_000_000


def dot(a, b):
    return jnp.dot(a, b, preferred_element_type=F32)


def rows_of(index, size):
    return pl.ds(pl.multiple_of(index * size, size), size)


def fold(x, op):
    return op(x.reshape(x.shape[0] // 8, 8, x.shape[1]), axis=0)


def ctx_peer(me, step):
    x = (me + step) % 4
    y = (me // 4 + step // 4) % 4
    z = (me // 16 + step // 16) % 2
    return z * 16 + y * 4 + x


def block_kernel(
    devices, parts, groups, q, k, v, ig, og, gm, w,
    dq_t, dk_t, dv_t, gi_t, fil_t, partials,
    qh, kh, vh, igh, gf, wf, gfp, xp, g, gg, later, earlier, kt, vt, s_all, dp_all, dka, dva, ot, dqt, corr,
    dq, gi, fil, gw,
    in_send, in_recv, in_own, out_send, out_recv, out_own, send_small, recv_small, own_small,
):
    me, part_id = lax.axis_index("ctx"), lax.axis_index("dp")
    local = q.shape[0]
    tokens, width = qh.shape
    tile = later.shape[1] // 2
    few = groups
    per = width // groups
    block, part = QUERY_BLOCK, KEY_ROWS
    blocks = tokens // block
    pieces = block // part
    targets = block // local
    scale = width**-0.5
    factor = scale * math.log2(math.e)

    barrier = pltpu.get_barrier_semaphore()

    def signal(step, carry):
        peer = ctx_peer(me, step // parts)
        other = (part_id + step) % parts
        pl.semaphore_signal(barrier, inc=1, device_id={"ctx": peer, "dp": other}, device_id_type=MESH)
        return carry

    lax.fori_loop(1, devices * parts, signal, 0)

    def gate(index, carry):
        at = rows_of(index, LANES)
        gf[:, at] = (gm[:, at].astype(F32) * og[:, at].astype(F32)).astype(BF16)
        return carry

    lax.fori_loop(0, devices, gate, 0)

    wf[...] = w[...].astype(F32)
    taps = wf[rows_of(me, groups), :]
    row = lax.broadcasted_iota(jnp.int32, (tile, tile), 0)
    col = lax.broadcasted_iota(jnp.int32, (tile, tile), 1)
    for n in range(groups):
        ring = jnp.broadcast_to(taps[n : n + 1, :], (tile, tile))
        shift = 1
        while shift < tile:
            ring = jnp.where((row & shift) != 0, pltpu.roll(ring, shift, 1), ring)
            shift *= 2
        upper = jnp.where(col >= row, ring, 0.0)
        lower = jnp.where(col < row, ring, 0.0)
        at = pl.ds(n * tile, tile)
        later[at, :tile] = upper.astype(BF16)
        later[at, tile:] = lower.astype(BF16)
        earlier[at, :tile] = lower.T.astype(BF16)
        earlier[at, tile:] = upper.T.astype(BF16)
    gfp[tokens:, :] = jnp.zeros((tile, width), BF16)
    xp[:tile, :] = jnp.zeros((tile, width), BF16)
    corr[...] = jnp.zeros_like(corr)

    pl.semaphore_wait(barrier, devices * parts - 1)

    mine = rows_of(me, local)
    incoming = ((gf, gfp), (ig, igh), (k, kh), (q, qh), (v, vh))
    for n, (src, dst) in enumerate(incoming):

        def send(step, carry, n=n, src=src, dst=dst):
            peer = ctx_peer(me, step)
            pltpu.make_async_remote_copy(
                src_ref=src.at[:, rows_of(peer, LANES)],
                dst_ref=dst.at[mine, :],
                send_sem=in_send.at[n],
                recv_sem=in_recv.at[n],
                device_id={"ctx": peer},
                device_id_type=MESH,
            ).start()
            return carry

        lax.fori_loop(1, devices, send, 0)
    own_in = [
        pltpu.make_async_copy(src.at[:, rows_of(me, LANES)], dst.at[mine, :], in_own.at[n])
        for n, (src, dst) in enumerate(incoming)
    ]
    for copy in own_in:
        copy.start()

    def arrived(n):
        own_in[n].wait()
        others = incoming[n][1].at[pl.ds(0, (devices - 1) * local), :]
        pltpu.make_async_copy(others, others, in_recv.at[n]).wait()

    lane_group = lax.broadcasted_iota(jnp.int32, (tile, width), 1) // per

    def convolved(matrix, signal, first):
        window = jnp.concatenate(
            [signal[pl.ds(pl.multiple_of(first + n * tile, tile), 2 * tile), :] for n in range(2)],
            axis=1,
        )
        result = [jnp.zeros((tile, width), F32)] * 2
        for n in range(groups):
            product = dot(matrix[pl.ds(n * tile, tile), :], window)
            for m in range(2):
                result[m] = jnp.where(lane_group == n, product[:, m * width : (m + 1) * width], result[m])
        return result

    def conv_back(index, carry):
        for m, value in enumerate(convolved(later, gfp, index * 2 * tile)):
            at = pl.ds(pl.multiple_of(index * 2 * tile + m * tile, tile), tile)
            gg[at, :] = value
            g[at, :] = (value * igh[at, :].astype(F32)).astype(BF16)
        return carry

    def turn(src, dst):
        def one(index, carry):
            dst[index] = src[rows_of(index, part), :].T
            return carry

        lax.fori_loop(0, tokens // part, one, 0)

    arrived(0)
    arrived(1)
    lax.fori_loop(0, tokens // (2 * tile), conv_back, 0)
    arrived(2)
    turn(kh, kt)
    arrived(3)

    row_group = lax.broadcasted_iota(jnp.int32, (width, tile), 0) // per

    def conv_ahead(index, carry):
        for m, value in enumerate(convolved(earlier, xp, index * 2 * tile)):
            at = pl.ds(pl.multiple_of(index * 2 * tile + m * tile, tile), tile)
            fil[at, :] = value.astype(BF16)
        lefts, rights = [], []
        for m in range(2):
            first = pl.multiple_of(index * 2 * tile + m * tile, tile)
            lefts.append(xp[pl.ds(first, 2 * tile), :])
            turned = gfp[pl.ds(first, tile), :].astype(F32).T
            rights.append(
                jnp.concatenate([jnp.where(row_group == n, turned, 0.0) for n in range(groups)], axis=1)
            )
        left = jnp.concatenate(lefts, axis=1)
        right = jnp.concatenate(rights, axis=0).astype(BF16)
        corr[...] += dot(left, right)
        return carry

    def conv_ahead_block(i):
        steps = block // (2 * tile)
        lax.fori_loop(i * steps, (i + 1) * steps, conv_ahead, 0)

    outgoing = ((dq, dq_t), (gi, gi_t), (fil, fil_t), (kh, dk_t), (vh, dv_t))
    columns = rows_of(me, LANES)

    def send_block(n, i):
        src, dst = outgoing[n]

        def one(step, carry):
            peer = i * targets + (me + step) % targets

            @pl.when(peer != me)
            def _():
                pltpu.make_async_remote_copy(
                    src_ref=src.at[rows_of(peer, local), :],
                    dst_ref=dst.at[:, columns],
                    send_sem=out_send.at[n],
                    recv_sem=out_recv.at[n],
                    device_id={"ctx": peer},
                    device_id_type=MESH,
                ).start()

            return carry

        lax.fori_loop(0, targets, one, 0)

    def send_all(n):
        src, dst = outgoing[n]

        def one(step, carry):
            peer = ctx_peer(me, step)
            pltpu.make_async_remote_copy(
                src_ref=src.at[rows_of(peer, local), :],
                dst_ref=dst.at[:, columns],
                send_sem=out_send.at[n],
                recv_sem=out_recv.at[n],
                device_id={"ctx": peer},
                device_id_type=MESH,
            ).start()
            return carry

        lax.fori_loop(1, devices, one, 0)

    def query_block(turn_id, carry):
        i = (me + turn_id) % blocks
        rows = rows_of(i, block)
        qb, gb = qh[rows, :], g[rows, :]
        q_t, g_t = qb.T, gb.T

        def key_rows(j, r):
            return pl.ds(pl.multiple_of(j * block + r * part, part), part)

        def widen(value, skip, fill):
            if skip == 0:
                return value
            return jnp.concatenate([jnp.full((value.shape[0], skip), fill, F32), value], axis=1)

        def scores(j, top, diagonal=False):
            for r in range(pieces):
                at = key_rows(j, r)
                skip = r * part if diagonal else 0
                s = dot(kh[at, :], q_t[:, skip:])
                if diagonal:
                    key_id = lax.broadcasted_iota(jnp.int32, s.shape, 0)
                    query_id = lax.broadcasted_iota(jnp.int32, s.shape, 1)
                    s = jnp.where(key_id <= query_id, s, -jnp.inf)
                s_all[at, skip:] = s
                top = jnp.maximum(top, widen(fold(s, jnp.max), skip, -jnp.inf))
            return top

        top = lax.fori_loop(0, i, scores, jnp.full((8, block), -jnp.inf, F32))
        top = jnp.max(scores(i, top, True), axis=0, keepdims=True)

        @pl.when(turn_id == 0)
        def _():
            arrived(4)
            turn(vh, vt)

        @pl.when(turn_id > 0)
        def _():
            before = (me + turn_id - 1) % blocks
            send_block(0, before)
            send_block(1, before)

        @pl.when(turn_id > 1)
        def _():
            send_block(2, (me + turn_id - 1) % blocks)

        def probs(j, sums, diagonal=False):
            total, inner = sums
            for r in range(pieces):
                at = key_rows(j, r)
                skip = r * part if diagonal else 0
                p = jnp.exp2((s_all[at, skip:] - top[:, skip:]) * factor)
                grad_p = dot(vh[at, :], g_t[:, skip:])
                s_all[at, skip:] = p
                dp_all[at, skip:] = grad_p
                total = total + widen(fold(p, jnp.sum), skip, 0.0)
                inner = inner + widen(fold(p * grad_p, jnp.sum), skip, 0.0)
            return total, inner

        none = jnp.zeros((8, block), F32)
        total, inner = probs(i, lax.fori_loop(0, i, probs, (none, none)), True)
        inverse = 1.0 / jnp.sum(total, axis=0, keepdims=True)
        inner = jnp.sum(inner, axis=0, keepdims=True) * inverse

        def grads(j, nothing, diagonal=False):
            for r in range(pieces):
                at = key_rows(j, r)
                skip = r * part if diagonal else 0
                p = s_all[at, skip:] * inverse[:, skip:]
                low = p.astype(BF16)
                grad_s = (p * (dp_all[at, skip:] - inner[:, skip:])).astype(BF16)
                dva[at, :] += dot(low, gb[skip:, :])
                dka[at, :] += dot(grad_s, qb[skip:, :])
                out_part = dot(vt[j * pieces + r], low)
                query_part = dot(kt[j * pieces + r], grad_s)
                if diagonal and r == 0:
                    ot[...] = out_part
                    dqt[...] = query_part
                else:
                    ot[:, skip:] += out_part
                    dqt[:, skip:] += query_part
            return nothing

        grads(i, 0, True)
        lax.fori_loop(0, i, grads, 0)
        attended = ot[...].T.astype(BF16).astype(F32)
        dq[rows, :] = (dqt[...] * scale).T.astype(BF16)
        gi[rows, :] = (gg[rows, :] * attended).astype(BF16)
        xp[pl.ds(pl.multiple_of(i * block + tile, tile), block), :] = (
            attended * igh[rows, :].astype(F32)
        ).astype(BF16)

        @pl.when(turn_id > 0)
        def _():
            conv_ahead_block(i)

        return carry

    dka[...] = jnp.zeros_like(dka)
    dva[...] = jnp.zeros_like(dva)
    lax.fori_loop(0, blocks, query_block, 0)

    def finish(index, carry):
        at = rows_of(index, part)
        kh[at, :] = (dka[at, :] * scale).astype(BF16)
        vh[at, :] = dva[at, :].astype(BF16)
        return carry

    lax.fori_loop(0, tokens // part, finish, 0)
    first_block, last_block = me % blocks, (me + blocks - 1) % blocks
    for n in range(3):
        send_block(n, last_block)
    send_all(3)
    send_all(4)
    conv_ahead_block(first_block)
    for n in range(groups):
        at = pl.ds(n * tile, tile)
        skewed = jnp.where(col >= row, corr[tile:, at], corr[:tile, at])
        shift = 1
        while shift < tile:
            skewed = jnp.where((row & shift) != 0, pltpu.roll(skewed, tile - shift, 1), skewed)
            shift *= 2
        gw[n : n + 1, :] = jnp.sum(skewed, axis=0, keepdims=True)
    send_block(2, first_block)

    small = partials.at[rows_of(part_id * devices + me, few), :]

    def send_partial(step, carry):
        peer = ctx_peer(me, step // parts)
        other = (part_id + step) % parts
        pltpu.make_async_remote_copy(
            src_ref=gw,
            dst_ref=small,
            send_sem=send_small,
            recv_sem=recv_small,
            device_id={"ctx": peer, "dp": other},
            device_id_type=MESH,
        ).start()
        return carry

    lax.fori_loop(1, devices * parts, send_partial, 0)
    own_part = pltpu.make_async_copy(gw, small, own_small)
    own_part.start()
    own_out = [
        pltpu.make_async_copy(src.at[mine, :], dst.at[:, columns], out_own.at[n])
        for n, (src, dst) in enumerate(outgoing)
    ]
    for copy in own_out:
        copy.start()
    for copy in own_out:
        copy.wait()
    own_part.wait()
    for n, (_, dst) in enumerate(outgoing):
        others = dst.at[:, pl.ds(0, (devices - 1) * LANES)]
        pltpu.make_async_copy(others, others, out_recv.at[n]).wait()
        pltpu.make_async_copy(others, others, out_send.at[n]).wait()
    for n, (_, dst) in enumerate(incoming):
        others = dst.at[pl.ds(0, (devices - 1) * local), :]
        pltpu.make_async_copy(others, others, in_send.at[n]).wait()
    others = partials.at[pl.ds(0, (devices * parts - 1) * few), :]
    for sem in (recv_small, send_small):
        pltpu.make_async_copy(others, others, sem).wait()


def block(devices, parts, q, k, v, ig, og, gm, w):
    local, channels = q.shape
    tokens, width = local * devices, channels // devices
    groups, tile = w.shape[0] // devices, w.shape[1]
    part = KEY_ROWS
    hbm = pl.BlockSpec(memory_space=pl.ANY)
    vmem = pl.BlockSpec(memory_space=pltpu.VMEM)
    rows = jax.ShapeDtypeStruct((local, channels), BF16)
    head = pltpu.VMEM((tokens, width), BF16)
    padded = pltpu.VMEM((tokens + tile, width), BF16)
    wide = pltpu.VMEM((tokens, width), F32)
    return pl.pallas_call(
        functools.partial(block_kernel, devices, parts, groups),
        out_shape=(rows,) * 5 + (jax.ShapeDtypeStruct((parts * w.shape[0], tile), F32),),
        in_specs=[hbm] * 4 + [vmem] * 3,
        out_specs=(hbm,) * 6,
        scratch_shapes=[
            head, head, head, head,
            pltpu.VMEM((local, channels), BF16),
            pltpu.VMEM(w.shape, F32),
            padded, padded, head, wide,
            pltpu.VMEM((groups * tile, 2 * tile), BF16),
            pltpu.VMEM((groups * tile, 2 * tile), BF16),
            pltpu.VMEM((tokens // part, width, part), BF16),
            pltpu.VMEM((tokens // part, width, part), BF16),
            pltpu.VMEM((tokens, QUERY_BLOCK), F32),
            pltpu.VMEM((tokens, QUERY_BLOCK), F32),
            wide, wide,
            pltpu.VMEM((width, QUERY_BLOCK), F32),
            pltpu.VMEM((width, QUERY_BLOCK), F32),
            pltpu.VMEM((2 * tile, groups * tile), F32),
            head, head, head,
            pltpu.VMEM((groups, tile), F32),
        ]
        + [pltpu.SemaphoreType.DMA((5,))] * 6
        + [pltpu.SemaphoreType.DMA] * 3,
        compiler_params=pltpu.CompilerParams(
            collective_id=0, has_side_effects=True, vmem_limit_bytes=VMEM_BYTES
        ),
        name="block",
    )(q, k, v, ig, og, gm, w)


def results_kernel(
    dq, dk, dv, gi, fil, parts, og, gm, out_block, out_q, out_k, out_v, out_outer, out_inner, out_w
):
    filtered = fil[...].astype(F32)
    out_block[...] = (og[...].astype(F32) * filtered).astype(BF16)
    out_outer[...] = (gm[...].astype(F32) * filtered).astype(BF16)
    out_q[...] = dq[...]
    out_k[...] = dk[...]
    out_v[...] = dv[...]
    out_inner[...] = gi[...]
    out_w[...] = jnp.sum(parts[...], axis=0)


def results(arrays, partials, og, gm):
    rows, channels = og.shape
    steps = 4
    wide = pl.BlockSpec((rows // steps, channels), lambda i: (i, 0))
    n_parts, few, taps = partials.shape
    array = jax.ShapeDtypeStruct((rows, channels), BF16)
    return pl.pallas_call(
        results_kernel,
        grid=(steps,),
        out_shape=(array,) * 6 + (jax.ShapeDtypeStruct((few, taps), F32),),
        in_specs=[wide] * 5
        + [pl.BlockSpec((n_parts, few // steps, taps), lambda i: (0, i, 0))]
        + [wide] * 2,
        out_specs=(wide,) * 6 + (pl.BlockSpec((few // steps, taps), lambda i: (i, 0)),),
        name="results",
    )(*arrays, partials, og, gm)


def on_device(queries, attn_keys, attn_values, outer_gate, inner_gate, conv_filter, grad_mixed):
    devices, parts = lax.axis_size("ctx"), lax.axis_size("dp")
    og, gm = outer_gate[0], grad_mixed[0]
    *arrays, partials = block(
        devices, parts, queries[0], attn_keys[0], attn_values[0], inner_gate[0], og, gm, conv_filter
    )
    partials = partials.reshape(parts, *conv_filter.shape)
    dq, dk, dv, gi, fil = arrays
    *arrays, grad_filter = results((dq, dk, dv, gi, fil), partials, og, gm)
    return (*[array[None] for array in arrays], grad_filter)


def solution(mesh):
    spread = P("dp", "ctx", None)
    return jax.shard_map(
        on_device,
        mesh=mesh,
        in_specs=(spread,) * 5 + (P(), spread),
        out_specs=(spread,) * 6 + (P(),),
        check_vma=False,
    )
```

```python
import functools
import math

import jax
import jax.numpy as jnp
from jax import lax
from jax.experimental import pallas as pl
from jax.experimental.pallas import tpu as pltpu
from jax.sharding import PartitionSpec as P

F32 = jnp.float32
BF16 = jnp.bfloat16
MESH = pl.DeviceIdType.MESH
LANES = 128
QUERY_BLOCK = 1024
KEY_ROWS = 256
VMEM_BYTES = 67_000_000


def dot(a, b):
    return jnp.dot(a, b, preferred_element_type=F32)


def rows_of(index, size):
    return pl.ds(pl.multiple_of(index * size, size), size)


def fold(x, op):
    return op(x.reshape(x.shape[0] // 8, 8, x.shape[1]), axis=0)


def ctx_peer(me, step):
    x = (me + step) % 4
    y = (me // 4 + step // 4) % 4
    z = (me // 16 + step // 16) % 2
    return z * 16 + y * 4 + x


def block_kernel(
    devices, parts, groups, q, k, v, ig, og, gm, w,
    dq_t, dk_t, dv_t, gi_t, fil_t, totals,
    qh, kh, vh, igh, gf, wf, gfp, xp, g, gg, later, earlier, kt, vt, s_all, dp_all, dka, dva, ot, dqt, corr,
    dq, gi, fil, gw, total_w,
    in_send, in_recv, in_own, out_send, out_recv, out_own, send_small, recv_small, own_small, share_send, share_recv,
):
    me, part_id = lax.axis_index("ctx"), lax.axis_index("dp")
    local = q.shape[0]
    tokens, width = qh.shape
    tile = later.shape[1] // 2
    few = groups
    per = width // groups
    block, part = QUERY_BLOCK, KEY_ROWS
    blocks = tokens // block
    pieces = block // part
    targets = block // local
    scale = width**-0.5
    factor = scale * math.log2(math.e)

    barrier = pltpu.get_barrier_semaphore()

    def signal(step, carry):
        pl.semaphore_signal(
            barrier, inc=1, device_id={"ctx": ctx_peer(me, step)}, device_id_type=MESH
        )
        return carry

    def signal_part(step, carry):
        pl.semaphore_signal(
            barrier, inc=1, device_id={"dp": (part_id + step) % parts}, device_id_type=MESH
        )
        return carry

    lax.fori_loop(1, devices, signal, 0)
    lax.fori_loop(1, parts, signal_part, 0)

    def gate(index, carry):
        at = rows_of(index, LANES)
        gf[:, at] = (gm[:, at].astype(F32) * og[:, at].astype(F32)).astype(BF16)
        return carry

    lax.fori_loop(0, devices, gate, 0)

    pl.semaphore_wait(barrier, devices + parts - 2)

    mine = rows_of(me, local)
    incoming = ((gf, gfp), (ig, igh), (k, kh), (q, qh), (v, vh))
    for n, (src, dst) in enumerate(incoming):

        def send(step, carry, n=n, src=src, dst=dst):
            peer = ctx_peer(me, step)
            pltpu.make_async_remote_copy(
                src_ref=src.at[:, rows_of(peer, LANES)],
                dst_ref=dst.at[mine, :],
                send_sem=in_send.at[n],
                recv_sem=in_recv.at[n],
                device_id={"ctx": peer},
                device_id_type=MESH,
            ).start()
            return carry

        lax.fori_loop(1, devices, send, 0)
    own_in = [
        pltpu.make_async_copy(src.at[:, rows_of(me, LANES)], dst.at[mine, :], in_own.at[n])
        for n, (src, dst) in enumerate(incoming)
    ]
    for copy in own_in:
        copy.start()

    wf[...] = w[...].astype(F32)
    taps = wf[rows_of(me, groups), :]
    row = lax.broadcasted_iota(jnp.int32, (tile, tile), 0)
    col = lax.broadcasted_iota(jnp.int32, (tile, tile), 1)
    for n in range(groups):
        ring = jnp.broadcast_to(taps[n : n + 1, :], (tile, tile))
        shift = 1
        while shift < tile:
            ring = jnp.where((row & shift) != 0, pltpu.roll(ring, shift, 1), ring)
            shift *= 2
        upper = jnp.where(col >= row, ring, 0.0)
        lower = jnp.where(col < row, ring, 0.0)
        at = pl.ds(n * tile, tile)
        later[at, :tile] = upper.astype(BF16)
        later[at, tile:] = lower.astype(BF16)
        earlier[at, :tile] = lower.T.astype(BF16)
        earlier[at, tile:] = upper.T.astype(BF16)
    gfp[tokens:, :] = jnp.zeros((tile, width), BF16)
    xp[:tile, :] = jnp.zeros((tile, width), BF16)
    corr[...] = jnp.zeros_like(corr)

    dka[...] = jnp.zeros_like(dka)
    dva[...] = jnp.zeros_like(dva)

    def arrived(n):
        own_in[n].wait()
        others = incoming[n][1].at[pl.ds(0, (devices - 1) * local), :]
        pltpu.make_async_copy(others, others, in_recv.at[n]).wait()

    lane_group = lax.broadcasted_iota(jnp.int32, (tile, width), 1) // per

    def convolved(matrix, signal, first):
        window = jnp.concatenate(
            [signal[pl.ds(pl.multiple_of(first + n * tile, tile), 2 * tile), :] for n in range(2)],
            axis=1,
        )
        result = [jnp.zeros((tile, width), F32)] * 2
        for n in range(groups):
            product = dot(matrix[pl.ds(n * tile, tile), :], window)
            for m in range(2):
                result[m] = jnp.where(lane_group == n, product[:, m * width : (m + 1) * width], result[m])
        return result

    def conv_back(index, carry):
        for m, value in enumerate(convolved(later, gfp, index * 2 * tile)):
            at = pl.ds(pl.multiple_of(index * 2 * tile + m * tile, tile), tile)
            gg[at, :] = value
            g[at, :] = (value * igh[at, :].astype(F32)).astype(BF16)
        return carry

    def turn(src, dst):
        def one(index, carry):
            dst[index] = src[rows_of(index, part), :].T
            return carry

        lax.fori_loop(0, tokens // part, one, 0)

    arrived(0)
    arrived(1)
    lax.fori_loop(0, tokens // (2 * tile), conv_back, 0)
    arrived(2)
    turn(kh, kt)
    arrived(3)

    row_group = lax.broadcasted_iota(jnp.int32, (width, tile), 0) // per

    def conv_ahead(index, carry):
        for m, value in enumerate(convolved(earlier, xp, index * 2 * tile)):
            at = pl.ds(pl.multiple_of(index * 2 * tile + m * tile, tile), tile)
            fil[at, :] = value.astype(BF16)
        lefts, rights = [], []
        for m in range(2):
            first = pl.multiple_of(index * 2 * tile + m * tile, tile)
            lefts.append(xp[pl.ds(first, 2 * tile), :])
            turned = gfp[pl.ds(first, tile), :].astype(F32).T
            rights.append(
                jnp.concatenate([jnp.where(row_group == n, turned, 0.0) for n in range(groups)], axis=1)
            )
        left = jnp.concatenate(lefts, axis=1)
        right = jnp.concatenate(rights, axis=0).astype(BF16)
        corr[...] += dot(left, right)
        return carry

    def conv_ahead_block(i):
        steps = block // (2 * tile)
        lax.fori_loop(i * steps, (i + 1) * steps, conv_ahead, 0)

    outgoing = ((dq, dq_t), (gi, gi_t), (fil, fil_t), (kh, dk_t), (vh, dv_t))
    columns = rows_of(me, LANES)

    def send_block(n, i):
        src, dst = outgoing[n]

        def one(step, carry):
            peer = i * targets + (me + step) % targets

            @pl.when(peer != me)
            def _():
                pltpu.make_async_remote_copy(
                    src_ref=src.at[rows_of(peer, local), :],
                    dst_ref=dst.at[:, columns],
                    send_sem=out_send.at[n],
                    recv_sem=out_recv.at[n],
                    device_id={"ctx": peer},
                    device_id_type=MESH,
                ).start()

            return carry

        lax.fori_loop(0, targets, one, 0)

    def send_all(n):
        src, dst = outgoing[n]

        def one(step, carry):
            peer = ctx_peer(me, step)
            pltpu.make_async_remote_copy(
                src_ref=src.at[rows_of(peer, local), :],
                dst_ref=dst.at[:, columns],
                send_sem=out_send.at[n],
                recv_sem=out_recv.at[n],
                device_id={"ctx": peer},
                device_id_type=MESH,
            ).start()
            return carry

        lax.fori_loop(1, devices, one, 0)

    def query_block(turn_id, carry):
        i = (me + turn_id) % blocks
        rows = rows_of(i, block)
        qb, gb = qh[rows, :], g[rows, :]
        q_t, g_t = qb.T, gb.T

        def key_rows(j, r):
            return pl.ds(pl.multiple_of(j * block + r * part, part), part)

        def widen(value, skip, fill):
            if skip == 0:
                return value
            return jnp.concatenate([jnp.full((value.shape[0], skip), fill, F32), value], axis=1)

        def scores(j, top, diagonal=False):
            for r in range(pieces):
                at = key_rows(j, r)
                skip = r * part if diagonal else 0
                s = dot(kh[at, :], q_t[:, skip:])
                if diagonal:
                    key_id = lax.broadcasted_iota(jnp.int32, s.shape, 0)
                    query_id = lax.broadcasted_iota(jnp.int32, s.shape, 1)
                    s = jnp.where(key_id <= query_id, s, -jnp.inf)
                s_all[at, skip:] = s
                top = jnp.maximum(top, widen(fold(s, jnp.max), skip, -jnp.inf))
            return top

        top = lax.fori_loop(0, i, scores, jnp.full((8, block), -jnp.inf, F32))
        top = jnp.max(scores(i, top, True), axis=0, keepdims=True)

        @pl.when(turn_id == 0)
        def _():
            arrived(4)
            turn(vh, vt)

        @pl.when(turn_id > 0)
        def _():
            before = (me + turn_id - 1) % blocks
            send_block(0, before)
            send_block(1, before)

        @pl.when(turn_id > 1)
        def _():
            send_block(2, (me + turn_id - 1) % blocks)

        def probs(j, sums, diagonal=False):
            total, inner = sums
            for r in range(pieces):
                at = key_rows(j, r)
                skip = r * part if diagonal else 0
                p = jnp.exp2((s_all[at, skip:] - top[:, skip:]) * factor)
                grad_p = dot(vh[at, :], g_t[:, skip:])
                s_all[at, skip:] = p
                dp_all[at, skip:] = grad_p
                total = total + widen(fold(p, jnp.sum), skip, 0.0)
                inner = inner + widen(fold(p * grad_p, jnp.sum), skip, 0.0)
            return total, inner

        none = jnp.zeros((8, block), F32)
        total, inner = probs(i, lax.fori_loop(0, i, probs, (none, none)), True)
        inverse = 1.0 / jnp.sum(total, axis=0, keepdims=True)
        inner = jnp.sum(inner, axis=0, keepdims=True) * inverse

        def grads(j, nothing, diagonal=False):
            for r in range(pieces):
                at = key_rows(j, r)
                skip = r * part if diagonal else 0
                p = s_all[at, skip:] * inverse[:, skip:]
                low = p.astype(BF16)
                grad_s = (p * (dp_all[at, skip:] - inner[:, skip:])).astype(BF16)
                dva[at, :] += dot(low, gb[skip:, :])
                dka[at, :] += dot(grad_s, qb[skip:, :])
                out_part = dot(vt[j * pieces + r], low)
                query_part = dot(kt[j * pieces + r], grad_s)
                if diagonal and r == 0:
                    ot[...] = out_part
                    dqt[...] = query_part
                else:
                    ot[:, skip:] += out_part
                    dqt[:, skip:] += query_part
            return nothing

        grads(i, 0, True)
        lax.fori_loop(0, i, grads, 0)
        attended = ot[...].T.astype(BF16).astype(F32)
        dq[rows, :] = (dqt[...] * scale).T.astype(BF16)
        gi[rows, :] = (gg[rows, :] * attended).astype(BF16)
        xp[pl.ds(pl.multiple_of(i * block + tile, tile), block), :] = (
            attended * igh[rows, :].astype(F32)
        ).astype(BF16)

        @pl.when(turn_id > 0)
        def _():
            conv_ahead_block(i)

        return carry

    lax.fori_loop(0, blocks, query_block, 0)

    def finish(index, carry):
        at = rows_of(index, part)
        kh[at, :] = (dka[at, :] * scale).astype(BF16)
        vh[at, :] = dva[at, :].astype(BF16)
        return carry

    lax.fori_loop(0, tokens // part, finish, 0)
    first_block, last_block = me % blocks, (me + blocks - 1) % blocks
    for n in range(3):
        send_block(n, last_block)
    conv_ahead_block(first_block)
    for n in range(groups):
        at = pl.ds(n * tile, tile)
        skewed = jnp.where(col >= row, corr[tile:, at], corr[:tile, at])
        shift = 1
        while shift < tile:
            skewed = jnp.where((row & shift) != 0, pltpu.roll(skewed, tile - shift, 1), skewed)
            shift *= 2
        gw[part_id, n : n + 1, :] = jnp.sum(skewed, axis=0, keepdims=True)
    send_all(3)

    def share(step, carry):
        pltpu.make_async_remote_copy(
            src_ref=gw.at[part_id],
            dst_ref=gw.at[part_id],
            send_sem=share_send,
            recv_sem=share_recv,
            device_id={"dp": (part_id + step) % parts},
            device_id_type=MESH,
        ).start()
        return carry

    lax.fori_loop(1, parts, share, 0)
    send_all(4)
    send_block(2, first_block)
    shared = gw.at[pl.ds(0, parts - 1)]
    pltpu.make_async_copy(shared, shared, share_recv).wait()
    total_w[...] = jnp.sum(gw[...], axis=0)
    small = totals.at[rows_of(me, few), :]

    def send_total(step, carry):
        pltpu.make_async_remote_copy(
            src_ref=total_w,
            dst_ref=small,
            send_sem=send_small,
            recv_sem=recv_small,
            device_id={"ctx": ctx_peer(me, step)},
            device_id_type=MESH,
        ).start()
        return carry

    lax.fori_loop(1, devices, send_total, 0)
    own_part = pltpu.make_async_copy(total_w, small, own_small)
    own_part.start()
    own_out = [
        pltpu.make_async_copy(src.at[mine, :], dst.at[:, columns], out_own.at[n])
        for n, (src, dst) in enumerate(outgoing)
    ]
    for copy in own_out:
        copy.start()
    for copy in own_out:
        copy.wait()
    own_part.wait()
    for n, (_, dst) in enumerate(outgoing):
        others = dst.at[:, pl.ds(0, (devices - 1) * LANES)]
        pltpu.make_async_copy(others, others, out_recv.at[n]).wait()
        pltpu.make_async_copy(others, others, out_send.at[n]).wait()
    for n, (_, dst) in enumerate(incoming):
        others = dst.at[pl.ds(0, (devices - 1) * local), :]
        pltpu.make_async_copy(others, others, in_send.at[n]).wait()
    pltpu.make_async_copy(shared, shared, share_send).wait()
    others = totals.at[pl.ds(0, (devices - 1) * few), :]
    for sem in (recv_small, send_small):
        pltpu.make_async_copy(others, others, sem).wait()


def block(devices, parts, q, k, v, ig, og, gm, w):
    local, channels = q.shape
    tokens, width = local * devices, channels // devices
    groups, tile = w.shape[0] // devices, w.shape[1]
    part = KEY_ROWS
    hbm = pl.BlockSpec(memory_space=pl.ANY)
    vmem = pl.BlockSpec(memory_space=pltpu.VMEM)
    rows = jax.ShapeDtypeStruct((local, channels), BF16)
    head = pltpu.VMEM((tokens, width), BF16)
    padded = pltpu.VMEM((tokens + tile, width), BF16)
    wide = pltpu.VMEM((tokens, width), F32)
    return pl.pallas_call(
        functools.partial(block_kernel, devices, parts, groups),
        out_shape=(rows,) * 5 + (jax.ShapeDtypeStruct(w.shape, F32),),
        in_specs=[hbm] * 4 + [vmem] * 3,
        out_specs=(hbm,) * 6,
        scratch_shapes=[
            head, head, head, head,
            pltpu.VMEM((local, channels), BF16),
            pltpu.VMEM(w.shape, F32),
            padded, padded, head, wide,
            pltpu.VMEM((groups * tile, 2 * tile), BF16),
            pltpu.VMEM((groups * tile, 2 * tile), BF16),
            pltpu.VMEM((tokens // part, width, part), BF16),
            pltpu.VMEM((tokens // part, width, part), BF16),
            pltpu.VMEM((tokens, QUERY_BLOCK), F32),
            pltpu.VMEM((tokens, QUERY_BLOCK), F32),
            wide, wide,
            pltpu.VMEM((width, QUERY_BLOCK), F32),
            pltpu.VMEM((width, QUERY_BLOCK), F32),
            pltpu.VMEM((2 * tile, groups * tile), F32),
            head, head, head,
            pltpu.VMEM((parts, groups, tile), F32),
            pltpu.VMEM((groups, tile), F32),
        ]
        + [pltpu.SemaphoreType.DMA((5,))] * 6
        + [pltpu.SemaphoreType.DMA] * 5,
        compiler_params=pltpu.CompilerParams(
            collective_id=0, has_side_effects=True, vmem_limit_bytes=VMEM_BYTES
        ),
        name="block",
    )(q, k, v, ig, og, gm, w)


def results_kernel(
    dq, dk, dv, gi, fil, totals, og, gm, out_block, out_q, out_k, out_v, out_outer, out_inner, out_w
):
    filtered = fil[...].astype(F32)
    out_block[...] = (og[...].astype(F32) * filtered).astype(BF16)
    out_outer[...] = (gm[...].astype(F32) * filtered).astype(BF16)
    out_q[...] = dq[...]
    out_k[...] = dk[...]
    out_v[...] = dv[...]
    out_inner[...] = gi[...]
    out_w[...] = totals[...]


def results(arrays, totals, og, gm):
    rows, channels = og.shape
    steps = 4
    wide = pl.BlockSpec((rows // steps, channels), lambda i: (i, 0))
    few, taps = totals.shape
    array = jax.ShapeDtypeStruct((rows, channels), BF16)
    return pl.pallas_call(
        results_kernel,
        grid=(steps,),
        out_shape=(array,) * 6 + (jax.ShapeDtypeStruct((few, taps), F32),),
        in_specs=[wide] * 5
        + [pl.BlockSpec((few // steps, taps), lambda i: (i, 0))]
        + [wide] * 2,
        out_specs=(wide,) * 6 + (pl.BlockSpec((few // steps, taps), lambda i: (i, 0)),),
        name="results",
    )(*arrays, totals, og, gm)


def on_device(queries, attn_keys, attn_values, outer_gate, inner_gate, conv_filter, grad_mixed):
    devices, parts = lax.axis_size("ctx"), lax.axis_size("dp")
    og, gm = outer_gate[0], grad_mixed[0]
    *arrays, totals = block(
        devices, parts, queries[0], attn_keys[0], attn_values[0], inner_gate[0], og, gm, conv_filter
    )
    dq, dk, dv, gi, fil = arrays
    *arrays, grad_filter = results((dq, dk, dv, gi, fil), totals, og, gm)
    return (*[array[None] for array in arrays], grad_filter)


def solution(mesh):
    spread = P("dp", "ctx", None)
    return jax.shard_map(
        on_device,
        mesh=mesh,
        in_specs=(spread,) * 5 + (P(), spread),
        out_specs=(spread,) * 6 + (P(),),
        check_vma=False,
    )
```
